32 devices in a mesh: grp: 4 (over x, core), blk: 8 (over z, y).
Axes of the slice: x: 2, y: 2, z: 4, core: 2. Of those that a mesh axis runs over, the one named last changes fastest.
Arguments:
- fine_coef: float32 [128, 20, 32, 128], P(('grp', 'blk')), may hold values from -6 to 6
- src_fine: int32 [256], P(('grp', 'blk')), may hold values from 0 to 3
- target_group: int32 [256], P(('grp', 'blk')), may hold values from 0 to 4, as said below
- slot: int32 [256], P(('grp', 'blk')), may hold values from 0 to 15
- valence_intersection: float32 [512, 20, 20], P(('grp', 'blk')), may hold values from -0.5 to 0.5
- conduction_intersection: float32 [512, 32, 32], P(('grp', 'blk')), may hold values from -1 to 1
- kernel: float32 [32, 4, 640, 640], P(('grp', 'blk')), may hold values from -0.125 to 0.125
- energies: float32 [32, 640], P(('grp', 'blk')), may hold values from 0.5 to 2
Outputs:
- applied: float32 [32, 640, 128], P(('grp', 'blk'))
The draws below stay inside these ranges and needn't reach their ends.
Inputs may be any that keep to these rules, and one draw needn't show every extreme that they name: `src_fine`: an index among the 4 fine momenta of the device that holds the entry. `slot`: an index among the 16 intersection slots of the device that holds the entry. `target_group`: the value 4 marks an unused entry; in each device's 8 entries the used ones come first, at least 2 of them, and some device uses all.
All inputs are finite; a program needn't handle non-finite values.
Results may differ from the reference program's by a relative error of at most 0.0003.
Values sent between devices are 32-bit elements; how exact they have to be, the bound alone decides.
No kernel may reach another device: no remote copies, remote signals or barrier semaphores. Data moves between devices by JAX's collectives and lax.ppermute only.
A program may use at most 64 MiB of HBM per device.

```python
import math
import jax
import jax.numpy as jnp
from jax import lax

NV = 20
NC = 32
NVEC = 128
STOPS = 4
F_DEV = 4
E_DEV = 8
W_DEV = 16
PAIRS = 640
FINE = 128
ENTRIES = 256
SLOTS = 512
NQ = 32
N_GRP = 4
N_BLK = 8
DEVICES = 32


def draw_target_group(key, part):
    first_key, second_key = jax.random.split(jax.random.fold_in(key, 11))
    chosen = jax.random.randint(first_key, (DEVICES, E_DEV), 0, N_GRP)
    used = jax.random.randint(second_key, (DEVICES,), E_DEV // 4, E_DEV + 1)
    used = used.at[0].set(E_DEV)
    position = jnp.arange(E_DEV, dtype=jnp.int32)[None, :]
    marked = jnp.where(position < used[:, None], chosen, N_GRP)
    return marked.reshape(DEVICES * E_DEV).astype(jnp.int32)


def place_ends(result, rng, least, high):
    place = [jax.random.randint(jax.random.fold_in(rng, axis), (), 0, length) for axis, length in enumerate(result.shape)]
    longest = result.shape.index(max(result.shape))
    next_to = place[:longest] + [(place[longest] + 1) % result.shape[longest]] + place[longest + 1:]
    return result.at[tuple(place)].set(least).at[tuple(next_to)].set(high)


def levels(key, dims, cuts, low, high):
    level = 1.0
    for axis_at, parts in cuts:
        steps = jax.random.uniform(jax.random.fold_in(jax.random.fold_in(key, 6), axis_at), (parts,), jnp.float32, low / len(cuts), high / len(cuts))
        level = level * jnp.repeat(jnp.exp(steps), dims[axis_at] // parts).reshape((-1,) + (1,) * (len(dims) - 1 - axis_at))
    return level


def normal_values(stream_key, extent, spread, reach, shards=(), held_as=jnp.bfloat16):
    array = jax.random.normal(stream_key, extent, jnp.float32) * spread
    if len(shards) > 0:
        array = levels(stream_key, extent, shards, -0.22, 0.18) * array
    return jnp.clip(array, min=-reach, max=reach).astype(held_as)


def setup_inputs(seed: int = 0) -> dict:
    keys = jax.random.split(jax.random.key(seed), 9)
    fine_coef = normal_values(keys[0], (FINE, NV, NC, NVEC), 1.0, 6.0, ((0, 32),), jnp.float32)
    src_fine = place_ends(jax.random.randint(keys[1], (ENTRIES,), 0, F_DEV), jax.random.fold_in(keys[1], 1), 0, F_DEV - 1).astype(jnp.int32)
    target_group = draw_target_group(jax.random.fold_in(keys[8], 71), 0)
    slot = place_ends(jax.random.randint(keys[3], (ENTRIES,), 0, W_DEV), jax.random.fold_in(keys[3], 1), 0, W_DEV - 1).astype(jnp.int32)
    valence_intersection = normal_values(keys[4], (SLOTS, NV, NV), (NV * E_DEV) ** -0.5, 0.5, ((0, 32),), jnp.float32)
    conduction_intersection = normal_values(keys[5], (SLOTS, NC, NC), NC ** -0.5, 1.0, ((0, 32),), jnp.float32)
    kernel = normal_values(keys[6], (NQ, STOPS, PAIRS, PAIRS), (STOPS * PAIRS) ** -0.5, 0.125, ((0, 32),), jnp.float32)
    energies = jnp.clip(jnp.exp(math.log(2.0) - 1.3862944 * jax.random.uniform(keys[7], (NQ, PAIRS), jnp.float32) ** levels(keys[7], (NQ, PAIRS), ((0, 32),), -0.2, 0.2)), 0.5, 2.0)
    return dict(fine_coef=fine_coef, src_fine=src_fine, target_group=target_group, slot=slot, valence_intersection=valence_intersection, conduction_intersection=conduction_intersection, kernel=kernel, energies=energies)


def rotate_entries(fine_part, src_part, target_part, slot_part, valence_part, conduction_part):
    entries = src_part.shape[0]
    block_size = 8
    src_rows = src_part.reshape(entries // block_size, block_size)
    target_rows = target_part.reshape(entries // block_size, block_size)
    slot_rows = slot_part.reshape(entries // block_size, block_size)
    totals = jnp.zeros((N_GRP, NV, NC, NVEC), jnp.float32)

    def advance(totals, pieces):
        src_now, target_now, slot_now = pieces
        gathered = jnp.take(fine_part, src_now, axis=0).astype(jnp.float32)
        val_now = jnp.take(valence_part, slot_now, axis=0).astype(jnp.float32)
        cond_now = jnp.take(conduction_part, slot_now, axis=0).astype(jnp.float32)
        partial_value = jnp.einsum("evw,evcn->ewcn", val_now, gathered, precision=lax.Precision.HIGHEST)
        rotated = jnp.einsum("ecd,ewcn->ewdn", cond_now, partial_value, precision=lax.Precision.HIGHEST)
        selector = (target_now[:, None] == jnp.arange(N_GRP, dtype=jnp.int32)[None, :]).astype(jnp.float32)
        totals = totals + jnp.einsum("eg,ewdn->gwdn", selector, rotated, precision=lax.Precision.HIGHEST)
        return totals, None

    totals, unused = lax.scan(advance, totals, (src_rows, target_rows, slot_rows))
    return totals


def reference(fine_coef, src_fine, target_group, slot, valence_intersection, conduction_intersection, kernel, energies):
    coarse = jnp.zeros((N_BLK, N_GRP, NV, NC, NVEC), jnp.float32)

    def add_device(device, coarse):
        device = jnp.asarray(device).astype(jnp.int32)
        fine_part = lax.dynamic_slice_in_dim(fine_coef, (device * F_DEV).astype(jnp.int32), F_DEV, 0)
        src_part = lax.dynamic_slice_in_dim(src_fine, (device * E_DEV).astype(jnp.int32), E_DEV, 0)
        target_part = lax.dynamic_slice_in_dim(target_group, (device * E_DEV).astype(jnp.int32), E_DEV, 0)
        slot_part = lax.dynamic_slice_in_dim(slot, (device * E_DEV).astype(jnp.int32), E_DEV, 0)
        valence_part = lax.dynamic_slice_in_dim(valence_intersection, (device * W_DEV).astype(jnp.int32), W_DEV, 0)
        conduction_part = lax.dynamic_slice_in_dim(conduction_intersection, (device * W_DEV).astype(jnp.int32), W_DEV, 0)
        totals = rotate_entries(fine_part, src_part, target_part, slot_part, valence_part, conduction_part)
        column = (device % N_BLK).astype(jnp.int32)
        return coarse.at[column].add(totals)

    coarse = lax.fori_loop(0, N_GRP * N_BLK, add_device, coarse)
    coarse = jnp.transpose(coarse, (1, 0, 2, 3, 4)).reshape(N_GRP, N_BLK, NV * NC, NVEC)
    flat = coarse.reshape(N_GRP * N_BLK, NV * NC, NVEC)
    applied = energies.astype(jnp.float32)[:, :, None] * flat
    for offset in range(STOPS):
        moved = jnp.roll(coarse, offset, axis=1).reshape(N_GRP * N_BLK, NV * NC, NVEC)
        applied = applied + jnp.einsum("qpr,qrn->qpn", kernel[:, offset].astype(jnp.float32), moved, precision=lax.Precision.HIGHEST)
    return applied
```

```python
import functools

import jax
import jax.numpy as jnp
from jax import lax
from jax.experimental import pallas as pl
from jax.experimental.pallas import tpu as pltpu
from jax.sharding import PartitionSpec as P

F32, BF16 = jnp.float32, jnp.bfloat16
LANES = 128


def moved(value, axis, target_of):
    count = lax.axis_size(axis)
    return lax.ppermute(value, axis, [(source, target_of(source)) for source in range(count)])


def split(value):
    high = value.astype(BF16)
    low = (value - high.astype(F32)).astype(BF16)
    return high, low


def dot_first(left, right):
    return lax.dot_general(left, right, (((0,), (0,)), ((), ())), preferred_element_type=F32)


def rotate_kernel(
    sizes, cuts, src, target, slot, group, x_ref, val_ref, cond_ref, *rest
):
    groups, order, entries, fine, slots, val, cond, vec = sizes
    outs, (stage, fine_rows, turned, total) = rest[: 2 * len(cuts)], rest[2 * len(cuts) :]
    pad = stage.shape[0]
    block = val * cond
    stage[...] = jnp.zeros_like(stage)
    for f in range(fine):
        for c in range(cond):
            stage[0:val, c * vec : (c + 1) * vec] = x_ref[pl.ds(f * block + c, val, stride=cond), :]
        high, low = split(stage[...])
        fine_rows[f, 0:pad] = high
        fine_rows[f, pad : 2 * pad] = high
        fine_rows[f, 2 * pad : 3 * pad] = low
    total[...] = jnp.zeros_like(total)

    def add_entry(e, carry):
        aim = target[e]

        @pl.when(aim < groups)
        def _():
            place = order(aim, group[0])
            which = slot[e]
            weights = val_ref[pl.ds(which, val, stride=slots), :]
            weights = jnp.concatenate([weights, jnp.zeros((pad - val, val), F32)], axis=0)
            high, low = split(weights)
            left = jnp.concatenate([high, low, high], axis=0)
            first = dot_first(left, fine_rows[src[e]])
            for c in range(cond):
                turned[pl.ds(c, val, stride=cond), :] = first[:, c * vec : (c + 1) * vec]
            wide = jnp.concatenate(
                [turned[w * cond : (w + 1) * cond, :] for w in range(val)], axis=1
            )
            high, low = split(wide)
            right = jnp.concatenate([high, high, low], axis=0)
            high, low = split(cond_ref[which])
            left = jnp.concatenate([high, low, high], axis=0)
            second = dot_first(left, right)
            for w in range(val):
                total[place, w * cond : (w + 1) * cond, :] += second[:, w * vec : (w + 1) * vec]

        return carry

    lax.fori_loop(0, entries, add_entry, 0)
    half = groups // 2
    for i, (start, width) in enumerate(cuts):
        outs[2 * i][...] = total[0:half, start : start + width, :]
        outs[2 * i + 1][...] = total[half:groups, start : start + width, :]


def apply_kernel(start, width, offsets, has_total, kernel_hbm, *rest):
    rest = list(rest)
    energies = rest.pop(0) if 0 in offsets else None
    total = rest.pop(0) if has_total else None
    values = [rest.pop(0) for _ in offsets]
    out, blocks, sems = rest
    copies = []
    for i, offset in enumerate(offsets):
        copy = pltpu.make_async_copy(
            kernel_hbm.at[0, offset, :, pl.ds(start, width)], blocks.at[i], sems.at[i]
        )
        copy.start()
        copies.append(copy)
    if has_total:
        out[...] = total[...]
    else:
        out[...] = jnp.zeros_like(out)
    for i, offset in enumerate(offsets):
        value = values[i][...]
        if offset == 0:
            for r in range(0, width, LANES):
                row = jnp.broadcast_to(
                    energies[0:1, start + r : start + r + LANES], (LANES, LANES)
                )
                out[start + r : start + r + LANES, :] += row.T * value[r : r + LANES, :]
        high, low = split(value)
        copies[i].wait()
        block_high, block_low = split(blocks[i])
        both = jnp.dot(
            block_high, jnp.concatenate([high, low], axis=1), preferred_element_type=F32
        )
        more = jnp.dot(block_low, high, preferred_element_type=F32)
        vec = value.shape[1]
        out[...] += both[:, :vec] + both[:, vec:] + more


def reversed_bits(value, bits):
    result = value * 0
    for k in range(bits):
        result = result + (((value >> k) & 1) << (bits - 1 - k))
    return result


def on_device(cuts_of, fine_coef, src, target, slot, valence, conduction, kernel, energies):
    groups = lax.axis_size("grp")
    fine, val, cond, vec = fine_coef.shape
    entries, slots = src.shape[0], valence.shape[0]
    bits = groups.bit_length() - 1
    cuts = cuts_of(val, cond)
    pairs = val * cond

    def order(aim, mine):
        return reversed_bits(aim ^ mine, bits)

    sizes = (groups, order, entries, fine, slots, val, cond, vec)
    pad = -(-val // 16) * 16
    vmem = pl.BlockSpec(memory_space=pltpu.VMEM)
    smem = pl.BlockSpec(memory_space=pltpu.SMEM)
    parts = pl.pallas_call(
        functools.partial(rotate_kernel, sizes, cuts),
        name="rotate",
        out_shape=[
            jax.ShapeDtypeStruct((groups // 2, width, vec), F32) for _, width in cuts for _ in range(2)
        ],
        in_specs=[smem] * 4 + [vmem] * 3,
        out_specs=[vmem] * (2 * len(cuts)),
        scratch_shapes=[
            pltpu.VMEM((pad, cond * vec), F32),
            pltpu.VMEM((fine, 3 * pad, cond * vec), BF16),
            pltpu.VMEM((pairs, vec), F32),
            pltpu.VMEM((groups, pairs, vec), F32),
        ],
        compiler_params=pltpu.CompilerParams(vmem_limit_bytes=32 << 20),
    )(
        src,
        target,
        slot,
        lax.axis_index("grp").astype(jnp.int32).reshape(1),
        fine_coef.reshape(fine * pairs, vec),
        jnp.transpose(valence, (1, 0, 2)).reshape(val * slots, val),
        conduction,
    )

    count = lax.axis_size("blk")
    result = None
    for i, (start, width) in enumerate(cuts):
        keep, give = parts[2 * i], parts[2 * i + 1]
        for bit in range(bits):
            keep = keep + moved(give, "grp", lambda source: source ^ (1 << bit))
            half = keep.shape[0] // 2
            if half > 0:
                keep, give = keep[:half], keep[half:]
        owned = keep[0]
        result = apply_part(result, kernel, energies, start, width, [0], [owned])
        offsets = list(range(1, kernel.shape[1]))
        values = [
            moved(owned, "blk", lambda source: (source + offset) % count) for offset in offsets
        ]
        result = apply_part(result, kernel, energies, start, width, offsets, values)
    return result[None]


def apply_part(total, kernel, energies, start, width, offsets, values):
    rows, vec = kernel.shape[2], values[0].shape[1]
    vmem = pl.BlockSpec(memory_space=pltpu.VMEM)
    operands = [kernel]
    specs = [pl.BlockSpec(memory_space=pl.ANY)]
    if 0 in offsets:
        operands.append(energies)
        specs.append(vmem)
    if total is not None:
        operands.append(total)
        specs.append(vmem)
    operands += values
    specs += [vmem] * len(values)
    return pl.pallas_call(
        functools.partial(apply_kernel, start, width, tuple(offsets), total is not None),
        name="apply",
        out_shape=jax.ShapeDtypeStruct((rows, vec), F32),
        in_specs=specs,
        out_specs=vmem,
        scratch_shapes=[
            pltpu.VMEM((len(offsets), rows, width), F32),
            pltpu.SemaphoreType.DMA((len(offsets),)),
        ],
        compiler_params=pltpu.CompilerParams(vmem_limit_bytes=24 << 20),
    )(*operands)


def cut_evenly(val, cond):
    return [(0, val * cond)]


def solution(mesh):
    spec = P(("grp", "blk"))
    return jax.shard_map(
        functools.partial(on_device, cut_evenly),
        mesh=mesh,
        in_specs=(spec,) * 8,
        out_specs=spec,
        check_vma=False,
    )
```

```python
import functools

import jax
import jax.numpy as jnp
from jax import lax
from jax.experimental import pallas as pl
from jax.experimental.pallas import tpu as pltpu
from jax.sharding import PartitionSpec as P


F32, BF16 = jnp.float32, jnp.bfloat16
LANES = 128
CHUNKS = 3


def moved(value, axis, target_of):
    count = lax.axis_size(axis)
    return lax.ppermute(value, axis, [(source, target_of(source)) for source in range(count)])


def kept(array):
    return pltpu.with_memory_space_constraint(array, pltpu.HBM)


def split(value):
    high = value.astype(BF16)
    low = (value - high.astype(F32)).astype(BF16)
    return high, low


def dot_first(left, right):
    return lax.dot_general(left, right, (((0,), (0,)), ((), ())), preferred_element_type=F32)


def rotate_kernel(
    sizes, cuts, group, *rest
):
    groups, order, entries, fine, slots, val, cond, vec = sizes
    given, outs, rest = rest[:6], rest[6 : 6 + 2 * len(cuts)], rest[6 + 2 * len(cuts) :]
    held, (stage, fine_rows, turned, total, sems) = rest[:6], rest[6:]
    copies = [pltpu.make_async_copy(a, b, sems.at[i]) for i, (a, b) in enumerate(zip(given, held))]
    for copy in copies:
        copy.start()
    src, target, slot, x_ref, val_ref, cond_ref = held
    total[...] = jnp.zeros_like(total)
    for copy in copies:
        copy.wait()
    pad = stage.shape[0]
    block = val * cond
    stage[...] = jnp.zeros_like(stage)
    for f in range(fine):
        for c in range(cond):
            stage[0:val, c * vec : (c + 1) * vec] = x_ref[pl.ds(f * block + c, val, stride=cond), :]
        high, low = split(stage[...])
        fine_rows[f, 0:pad] = high
        fine_rows[f, pad : 2 * pad] = high
        fine_rows[f, 2 * pad : 3 * pad] = low

    def add_entry(e, carry):
        aim = target[e]

        @pl.when(aim < groups)
        def _():
            place = order(aim, group[0])
            which = slot[e]
            weights = val_ref[pl.ds(which, val, stride=slots), :]
            weights = jnp.concatenate([weights, jnp.zeros((pad - val, val), F32)], axis=0)
            high, low = split(weights)
            left = jnp.concatenate([high, low, high], axis=0)
            first = dot_first(left, fine_rows[src[e]])
            for c in range(cond):
                turned[pl.ds(c, val, stride=cond), :] = first[:, c * vec : (c + 1) * vec]
            wide = jnp.concatenate(
                [turned[w * cond : (w + 1) * cond, :] for w in range(val)], axis=1
            )
            high, low = split(wide)
            right = jnp.concatenate([high, high, low], axis=0)
            high, low = split(cond_ref[which])
            left = jnp.concatenate([high, low, high], axis=0)
            second = dot_first(left, right)
            for w in range(val):
                total[place, w * cond : (w + 1) * cond, :] += second[:, w * vec : (w + 1) * vec]

        return carry

    lax.fori_loop(0, entries, add_entry, 0)
    half = groups // 2
    for i, (start, width) in enumerate(cuts):
        outs[2 * i][...] = total[0:half, start : start + width, :]
        outs[2 * i + 1][...] = total[half:groups, start : start + width, :]


def apply_kernel(start, width, offsets, has_total, kernel_hbm, *rest):
    rest = list(rest)
    energies = rest.pop(0) if 0 in offsets else None
    total = rest.pop(0) if has_total else None
    values = [rest.pop(0) for _ in offsets]
    out, blocks, levels, sems = rest
    copies = []
    if energies is not None:
        fetched = pltpu.make_async_copy(
            energies.at[:, pl.ds(start, width)], levels, sems.at[len(offsets)]
        )
        fetched.start()
    for i, offset in enumerate(offsets):
        copy = pltpu.make_async_copy(
            kernel_hbm.at[0, offset, :, pl.ds(start, width)], blocks.at[i], sems.at[i]
        )
        copy.start()
        copies.append(copy)
    if has_total:
        out[...] = total[...]
    else:
        out[...] = jnp.zeros_like(out)
    for i, offset in enumerate(offsets):
        value = values[i][...]
        if offset == 0:
            fetched.wait()
            for r in range(0, width, LANES):
                row = jnp.broadcast_to(
                    levels[0:1, r : r + LANES], (LANES, LANES)
                )
                out[start + r : start + r + LANES, :] += row.T * value[r : r + LANES, :]
        high, low = split(value)
        copies[i].wait()
        block_high, block_low = split(blocks[i])
        both = jnp.dot(
            block_high, jnp.concatenate([high, low], axis=1), preferred_element_type=F32
        )
        more = jnp.dot(block_low, high, preferred_element_type=F32)
        vec = value.shape[1]
        out[...] += both[:, :vec] + both[:, vec:] + more


def reversed_bits(value, bits):
    result = value * 0
    for k in range(bits):
        result = result + (((value >> k) & 1) << (bits - 1 - k))
    return result


def on_device(cuts_of, fine_coef, src, target, slot, valence, conduction, kernel, energies):
    groups = lax.axis_size("grp")
    fine, val, cond, vec = fine_coef.shape
    entries, slots = src.shape[0], valence.shape[0]
    bits = groups.bit_length() - 1
    cuts = cuts_of(val, cond)
    pairs = val * cond

    def order(aim, mine):
        return reversed_bits(aim ^ mine, bits)

    sizes = (groups, order, entries, fine, slots, val, cond, vec)
    pad = -(-val // 16) * 16
    vmem = pl.BlockSpec(memory_space=pltpu.VMEM)
    smem = pl.BlockSpec(memory_space=pltpu.SMEM)
    hbm = pl.BlockSpec(memory_space=pltpu.HBM)
    parts = pl.pallas_call(
        functools.partial(rotate_kernel, sizes, cuts),
        name="rotate",
        out_shape=[
            jax.ShapeDtypeStruct((groups // 2, width, vec), F32) for _, width in cuts for _ in range(2)
        ],
        in_specs=[smem] + [hbm] * 6,
        out_specs=[vmem] * (2 * len(cuts)),
        scratch_shapes=[
            pltpu.SMEM((entries,), jnp.int32),
            pltpu.SMEM((entries,), jnp.int32),
            pltpu.SMEM((entries,), jnp.int32),
            pltpu.VMEM((fine * pairs, vec), F32),
            pltpu.VMEM((val * slots, val), F32),
            pltpu.VMEM((slots, cond, cond), F32),
            pltpu.VMEM((pad, cond * vec), F32),
            pltpu.VMEM((fine, 3 * pad, cond * vec), BF16),
            pltpu.VMEM((pairs, vec), F32),
            pltpu.VMEM((groups, pairs, vec), F32),
            pltpu.SemaphoreType.DMA((6,)),
        ],
        compiler_params=pltpu.CompilerParams(vmem_limit_bytes=32 << 20),
    )(
        lax.axis_index("grp").astype(jnp.int32).reshape(1),
        kept(src),
        kept(target),
        kept(slot),
        kept(fine_coef.reshape(fine * pairs, vec)),
        kept(jnp.transpose(valence, (1, 0, 2)).reshape(val * slots, val)),
        kept(conduction),
    )

    owned = []
    for i in range(len(cuts)):
        keep, give = parts[2 * i], parts[2 * i + 1]
        for bit in range(bits):
            keep = keep + moved(give, "grp", lambda source: source ^ (1 << bit))
            half = keep.shape[0] // 2
            if half > 0:
                keep, give = keep[:half], keep[half:]
        owned.append(keep[0])
    result = None
    for (start, width), own in zip(cuts, owned):
        behind = shifted_back(own, kernel.shape[1])
        result = apply_part(result, kernel, energies, start, width, [0], [own])
        early = [s for s in behind if s < 3]
        late = [s for s in behind if s >= 3]
        for chosen in (early, late):
            if chosen:
                values = [behind[s] for s in chosen]
                result = apply_part(result, kernel, energies, start, width, chosen, values)
    return result[None]


def shifted_back(own, stops):
    count = lax.axis_size("blk")
    behind = {0: own}
    if count % 2 == 0 and stops > 2:
        odd = lax.axis_index("blk") % 2 == 1
        behind[2] = moved(own, "blk", lambda source: (source + 2) % count)
        mixed = jnp.where(odd, behind[2], own)
        behind[1] = moved(mixed, "blk", lambda source: source ^ 1)
    elif stops > 1:
        behind[1] = moved(own, "blk", lambda source: (source + 1) % count)
    for s in range(2, stops):
        if s not in behind:
            behind[s] = moved(behind[s - 2], "blk", lambda source: (source + 2) % count)
    del behind[0]
    return behind


def apply_part(total, kernel, energies, start, width, offsets, values):
    rows, vec = kernel.shape[2], values[0].shape[1]
    vmem = pl.BlockSpec(memory_space=pltpu.VMEM)
    operands = [kept(kernel)]
    specs = [pl.BlockSpec(memory_space=pltpu.HBM)]
    if 0 in offsets:
        operands.append(kept(energies))
        specs.append(specs[0])
    if total is not None:
        operands.append(total)
        specs.append(vmem)
    operands += values
    specs += [vmem] * len(values)
    return pl.pallas_call(
        functools.partial(apply_kernel, start, width, tuple(offsets), total is not None),
        name="apply",
        out_shape=jax.ShapeDtypeStruct((rows, vec), F32),
        in_specs=specs,
        out_specs=vmem,
        scratch_shapes=[
            pltpu.VMEM((len(offsets), rows, width), F32),
            pltpu.VMEM((1, width), F32),
            pltpu.SemaphoreType.DMA((len(offsets) + 1,)),
        ],
        compiler_params=pltpu.CompilerParams(vmem_limit_bytes=24 << 20),
    )(*operands)


def cut_evenly(val, cond):
    step = next(w for w in range(1, val + 1) if val % w == 0 and (w * cond % LANES == 0 or w == val))
    steps = val // step
    counts = [steps * (k + 1) // CHUNKS - steps * k // CHUNKS for k in range(CHUNKS)]
    cuts, start = [], 0
    for count in counts:
        if count:
            cuts.append((start * step * cond, count * step * cond))
            start += count
    return cuts


def solution(mesh):
    spec = P(("grp", "blk"))

    def body(*args):
        return on_device(cut_evenly, *args)

    return jax.shard_map(
        body, mesh=mesh, in_specs=(spec,) * 8, out_specs=spec, check_vma=False
    )
```

```python
import functools

import jax
import jax.numpy as jnp
from jax import lax
from jax.experimental import pallas as pl
from jax.experimental.pallas import tpu as pltpu
from jax.sharding import PartitionSpec as P


F32, BF16 = jnp.float32, jnp.bfloat16
LANES, SUBLANES = 128, 8
CHUNKS = 3


def moved(value, axis, target_of):
    count = lax.axis_size(axis)
    return lax.ppermute(value, axis, [(source, target_of(source)) for source in range(count)])


def kept(array):
    return pltpu.with_memory_space_constraint(array, pltpu.HBM)


def split(value):
    high = value.astype(BF16)
    low = (value - high.astype(F32)).astype(BF16)
    return high, low


def stacked(first, second, third):
    parts = [part.astype(F32) for part in (first, second, third)]
    rows = sum(part.shape[0] for part in parts)
    fill = -rows % (2 * SUBLANES)
    if fill:
        parts.append(jnp.zeros((fill, parts[0].shape[1]), F32))
    return jnp.concatenate(parts, axis=0).astype(BF16)


def dot_first(left, right):
    return lax.dot_general(left, right, (((0,), (0,)), ((), ())), preferred_element_type=F32)


def rotate_kernel(sizes, cuts, group, *rest):
    groups, order, entries, fine, slots, val, cond, vec = sizes
    given, rest = rest[:8], rest[8:]
    outs, rest = rest[: 2 * len(cuts)], rest[2 * len(cuts) :]
    late, rest = rest[:2], rest[2:]
    held, (fine_rows, total, sems) = rest[:6], rest[6:]
    copies = [
        pltpu.make_async_copy(a, b, sems.at[i]) for i, (a, b) in enumerate(zip(given, held + late))
    ]
    for copy in copies[:6]:
        copy.start()
    src, target, slot, x_ref, val_ref, cond_ref = held
    total[...] = jnp.zeros_like(total)
    for copy in copies[:6]:
        copy.wait()
    for copy in copies[6:]:
        copy.start()
    pad = -(-val // SUBLANES) * SUBLANES
    for f in range(fine):
        x = jnp.concatenate([x_ref[f], jnp.zeros((pad - val, cond, vec), F32)], axis=0)
        high, low = split(x.reshape(pad, cond * vec))
        fine_rows[f] = stacked(high, high, low)

    def add_entry(e, carry):
        aim = target[e]

        @pl.when(aim < groups)
        def _():
            place = order(aim, group[0])
            which = slot[e]
            weights = val_ref[pl.ds(which, val, stride=slots), :]
            weights = jnp.concatenate([weights, jnp.zeros((pad - val, val), F32)], axis=0)
            weights = jnp.concatenate([weights, jnp.zeros((pad, pad - val), F32)], axis=1)
            high, low = split(weights)
            first = dot_first(stacked(high, low, high), fine_rows[src[e]])
            turned = first.reshape(pad, cond, vec)
            wide = jnp.concatenate([turned[w] for w in range(val)], axis=1)
            high, low = split(wide)
            right = stacked(high, high, low)
            high, low = split(cond_ref[which])
            second = dot_first(stacked(high, low, high), right)
            for w in range(val):
                total[place, w * cond : (w + 1) * cond, :] += second[:, w * vec : (w + 1) * vec]

        return carry

    lax.fori_loop(0, entries, add_entry, 0)
    half = groups // 2
    for i, (start, width) in enumerate(cuts):
        outs[2 * i][...] = total[0:half, start : start + width, :]
        outs[2 * i + 1][...] = total[half:groups, start : start + width, :]
    for copy in copies[6:]:
        copy.wait()


def apply_kernel(terms, has_total, blocks, *rest):
    rest = list(rest)
    out = rest.pop()
    total = rest.pop(0) if has_total else None
    energies = None if has_total else rest.pop(0)
    if has_total:
        out[...] = total[...]
    for (offset, start), ref in zip(terms, rest):
        value = ref[...]
        width, vec = value.shape
        high, low = split(value)
        block_high, block_low = split(blocks[0, offset, :, start : start + width])
        both = jnp.dot(
            block_high, jnp.concatenate([high, low], axis=1), preferred_element_type=F32
        )
        both = both[:, :vec] + both[:, vec:]
        both = both + jnp.dot(block_low, high, preferred_element_type=F32)
        if energies is not None and start == 0:
            out[...] = both
        else:
            out[...] += both
    if energies is not None:
        for (_, start), ref in zip(terms, rest):
            step = min(LANES, ref.shape[0])
            for r in range(0, ref.shape[0], step):
                rows = pl.ds(start + r, step)
                level = jnp.broadcast_to(energies[0:1, start + r : start + r + step], (step, step))
                out[rows, :] += level.T[:, 0:1] * ref[r : r + step, :]


def reversed_bits(value, bits):
    result = value * 0
    for k in range(bits):
        result = result + (((value >> k) & 1) << (bits - 1 - k))
    return result


def shifted_back(own, stops, odd):
    count = lax.axis_size("blk")
    behind = {}
    if count % 2 == 0 and stops > 2:
        behind[2] = moved(own, "blk", lambda source: (source + 2) % count)
        mixed = jnp.where(odd, behind[2], own)
        behind[1] = moved(mixed, "blk", lambda source: source ^ 1)
    elif stops > 1:
        behind[1] = moved(own, "blk", lambda source: (source + 1) % count)
    before = {0: own, **behind}
    for s in range(2, stops):
        if s not in before:
            before[s] = moved(before[s - 2], "blk", lambda source: (source + 2) % count)
            behind[s] = before[s]
    return behind


def apply_part(total, blocks, energies, terms, values):
    rows, vec = blocks.shape[2], values[0].shape[1]
    vmem = pl.BlockSpec(memory_space=pltpu.VMEM)
    return pl.pallas_call(
        functools.partial(apply_kernel, tuple(terms), total is not None),
        name="apply",
        out_shape=jax.ShapeDtypeStruct((rows, vec), F32),
        in_specs=[vmem] * (2 + len(values)),
        out_specs=vmem,
        compiler_params=pltpu.CompilerParams(vmem_limit_bytes=24 << 20),
    )(blocks, energies if total is None else total, *values)


def on_device(cuts_of, fine_coef, src, target, slot, valence, conduction, kernel, energies):
    groups = lax.axis_size("grp")
    fine, val, cond, vec = fine_coef.shape
    entries, slots = src.shape[0], valence.shape[0]
    bits = groups.bit_length() - 1
    cuts = cuts_of(val, cond)
    pairs = val * cond

    def order(aim, mine):
        return reversed_bits(aim ^ mine, bits)

    sizes = (groups, order, entries, fine, slots, val, cond, vec)
    pad = -(-val // SUBLANES) * SUBLANES
    depth = -(-3 * pad // (2 * SUBLANES)) * 2 * SUBLANES
    vmem = pl.BlockSpec(memory_space=pltpu.VMEM)
    smem = pl.BlockSpec(memory_space=pltpu.SMEM)
    hbm = pl.BlockSpec(memory_space=pltpu.HBM)
    mine, odd = lax.optimization_barrier(
        (lax.axis_index("grp").astype(jnp.int32).reshape(1), (lax.axis_index("blk") & 1) == 1)
    )
    *parts, blocks, levels = pl.pallas_call(
        functools.partial(rotate_kernel, sizes, cuts),
        name="rotate",
        out_shape=[
            jax.ShapeDtypeStruct((groups // 2, width, vec), F32) for _, width in cuts for _ in range(2)
        ]
        + [
            jax.ShapeDtypeStruct(kernel.shape, F32),
            jax.ShapeDtypeStruct(energies.shape, F32),
        ],
        in_specs=[smem] + [hbm] * 8,
        out_specs=[vmem] * (2 * len(cuts) + 2),
        scratch_shapes=[
            pltpu.SMEM((entries,), jnp.int32),
            pltpu.SMEM((entries,), jnp.int32),
            pltpu.SMEM((entries,), jnp.int32),
            pltpu.VMEM((fine, val, cond, vec), F32),
            pltpu.VMEM((val * slots, val), F32),
            pltpu.VMEM((slots, cond, cond), F32),
            pltpu.VMEM((fine, depth, cond * vec), BF16),
            pltpu.VMEM((groups, pairs, vec), F32),
            pltpu.SemaphoreType.DMA((8,)),
        ],
        compiler_params=pltpu.CompilerParams(vmem_limit_bytes=32 << 20),
    )(
        mine,
        kept(src),
        kept(target),
        kept(slot),
        kept(fine_coef),
        kept(jnp.transpose(valence, (1, 0, 2)).reshape(val * slots, val)),
        kept(conduction),
        kept(kernel),
        kept(energies),
    )

    owned, behind = [], []
    for i in range(len(cuts)):
        keep, give = parts[2 * i], parts[2 * i + 1]
        for bit in range(bits):
            got = moved(give, "grp", lambda source: source ^ (1 << bit))
            keep = keep + got
            half = keep.shape[0] // 2
            if half > 0:
                keep, give = keep[:half], keep[half:]
            else:
                keep = keep[0]
        owned.append(keep)
        behind.append(shifted_back(keep, kernel.shape[1], odd))
    starts = [start for start, _ in cuts]
    result = apply_part(None, blocks, levels, [(0, start) for start in starts], owned)
    for i, start in enumerate(starts):
        near = [s for s in behind[i] if s < 3]
        if near:
            result = apply_part(
                result, blocks, None, [(s, start) for s in near], [behind[i][s] for s in near]
            )
    for i, start in enumerate(starts):
        far = [s for s in behind[i] if s >= 3]
        if far:
            result = apply_part(
                result, blocks, None, [(s, start) for s in far], [behind[i][s] for s in far]
            )
    return result[None]


def cut_evenly(val, cond):
    step = next(w for w in range(1, val + 1) if val % w == 0 and (w * cond % LANES == 0 or w == val))
    steps = val // step
    counts = [steps * (k + 1) // CHUNKS - steps * k // CHUNKS for k in range(CHUNKS)]
    cuts, start = [], 0
    for count in counts:
        if count:
            cuts.append((start * step * cond, count * step * cond))
            start += count
    return cuts


def solution(mesh):
    spec = P(("grp", "blk"))

    def body(*args):
        return on_device(cut_evenly, *args)

    return jax.shard_map(
        body, mesh=mesh, in_specs=(spec,) * 8, out_specs=spec, check_vma=False
    )
```
